32 devices in a mesh: row: 4 (over z), col: 8 (over y, x, core).
Axes of the slice: x: 2, y: 2, z: 4, core: 2. Of those that a mesh axis runs over, the one named last changes fastest.
Arguments:
- coords: float32 [16, 16384], replicated, may hold values from -8 to 8
- panel: bfloat16 [16384, 128], P(('row', 'col')), may hold values from -6 to 6
- mixing: float32 [128, 64], replicated, may hold values from -0.5 to 0.5
- owners: int32 [512, 1], P(('row', 'col')), may hold values from 0 to 31; in each aligned block of 16 rows (0 to 15, 16 to 31, ...) no two rows name the same one
- leaf_picks: int32 [512, 2], P(('row', 'col')), may hold values from 0 to 1
Outputs:
- bases: bfloat16 [64, 16384], P(('row', 'col'))
- couplings: float32 [512, 4096], P(('row', 'col'))
The draws below stay inside these ranges and needn't reach their ends.
Inputs may be any that keep to these rules, and one draw needn't show every extreme that they name: `owners`: among the 16 pairs of one device, no device is named more than 1 times, so the 16 pairs of a device name 16 distinct devices; every device is named somewhere.
All inputs are finite; a program needn't handle non-finite values.
Results may differ from the reference program's by a relative error of at most 0.011.
Values may be sent and summed in bfloat16 or wider, within the bound.
No kernel may reach another device: no remote copies, remote signals or barrier semaphores. Data moves between devices by JAX's collectives and lax.ppermute only.
A program may use at most 64 MiB of HBM per device.

```python
import math
import jax
import jax.numpy as jnp
import numpy as np
from jax import lax

PT_DEV = 512
LEAF = 256
RANK = 64
SKETCH = 128
DIM = 16
NSWEEPS = 6
CAP = 1
NPTS = 16384
LEAVES_DEV = 2
NLEAVES = 64
PAIRS_DEV = 16
NPAIRS = 512
DEVICES = 32


def draw_coords(key, part):
    key_center = jax.random.fold_in(key, 101)
    key_offset = jax.random.fold_in(key, 202)
    key_jitter = jax.random.fold_in(key, 303)
    centers = 0.7071 * jax.random.normal(key_center, (DIM, DEVICES), jnp.float32)
    offsets = 0.5 * jax.random.normal(key_offset, (DIM, NLEAVES), jnp.float32)
    jitter = 0.5 * jax.random.normal(key_jitter, (DIM, NPTS), jnp.float32)
    coords = jnp.repeat(centers, PT_DEV, axis=1) + jnp.repeat(offsets, LEAF, axis=1) + jitter
    return jnp.clip(coords, -8.0, 8.0)


def plant(result, rng, low, largest):
    shape = result.shape
    index_at = [jax.random.randint(jax.random.fold_in(rng, axis), (), 0, shape[axis]) for axis in range(len(shape))]
    result = result.at[tuple(index_at)].set(low)
    longest = shape.index(max(shape))
    index_at[longest] = (index_at[longest] + 1) % shape[longest]
    return result.at[tuple(index_at)].set(largest)


def level_of(own_key, dims, cuts, least, top_value):
    gain, own = 1.0, jax.random.fold_in(own_key, 6)
    for axis_at, parts in cuts:
        draws = jnp.exp(jax.random.uniform(jax.random.fold_in(own, axis_at), (parts,), jnp.float32, least / len(cuts), top_value / len(cuts)))
        gain = gain * jnp.repeat(draws, dims[axis_at] // parts).reshape([-1 if axis == axis_at else 1 for axis in range(len(dims))])
    return gain


def deal_out(stream_key, own, number, rows, count, top, reach, skew):
    ranking = jax.random.permutation(stream_key, count)
    packed, ordinary = portions_of(count, rows * top, reach, skew, True), portions_of(count, rows * top, reach, skew, False)
    places = jnp.arange(count)

    def named(lengths, offset_by):
        used = int((lengths > 0).sum())
        fixed = max(1, used // 4)
        passed = fixed + (places - fixed + offset_by * (used - fixed)) % max(1, count - fixed)
        return jnp.zeros((count,), jnp.int32).at[ranking[jnp.where(places < fixed, places, passed)]].set(jnp.asarray(lengths, jnp.int32))

    lengths = jnp.where(number % 4 == 0, named(packed, number // 4), named(ordinary, number - number // 4 - 1))
    mixed = jax.random.permutation(jax.random.fold_in(own, 3), count)
    source_of, sink = mixed[0:count // 2 * 2:2], mixed[1:count // 2 * 2:2]
    room = jnp.minimum(lengths[source_of] - 1, reach - lengths[sink]) // 2
    room = jnp.where((source_of == ranking[0]) | (sink == ranking[0]) | (lengths[sink] == 0), 0, jnp.maximum(room, 0))
    passed = jax.random.randint(jax.random.fold_in(own, 4), (count // 2,), 0, 1 << 20) % (room + 1)
    lengths = lengths.at[source_of].add(-passed).at[sink].add(passed)
    members = jnp.searchsorted(jnp.cumsum(lengths), jnp.arange(rows * top), side="right").astype(jnp.int32)
    grid = members.reshape(top, rows).T
    grid = grid[jax.random.permutation(jax.random.fold_in(own, 1), rows)]
    offset_by = jax.random.randint(jax.random.fold_in(own, 2), (rows, 1), 0, top)
    return jnp.take_along_axis(grid, (jnp.arange(top)[None, :] + offset_by) % top, axis=1)


def portions_of(count, total, reach, skew, full):
    loads = [(1 << 20) // math.isqrt(rank ** skew) + 1 for rank in range(1, count + 1)]
    largest = reach if full else min(reach, max(-(-total // count), total * loads[0] // sum(loads)))
    least = 1 if total - largest >= count - 1 else 0
    given, rest = [largest] + [least] * (count - 1), total - largest - least * (count - 1)
    while rest > 0:
        movable = [i for i in range(1, count) if given[i] < largest] or [i for i in range(1, count) if given[i] < reach]
        pool, left = sum([loads[i] for i in movable]), rest
        for i in movable:
            more = min(reach - given[i], max(1, left * loads[i] // pool), rest)
            given[i] = given[i] + more
            rest = rest - more
    return np.array(given)


def noise(own_key, dims, width, bound, cuts=(), kind=jnp.bfloat16):
    result = jax.random.normal(own_key, dims, jnp.float32) * width
    if len(cuts) > 0:
        result = level_of(own_key, dims, cuts, -0.22, 0.18) * result
    return jnp.clip(result, min=-bound, max=bound).astype(kind)


def setup_inputs(seed: int = 0) -> dict:
    keys = jax.random.split(jax.random.key(seed), 6)
    coords = draw_coords(jax.random.fold_in(keys[5], 71), 0)
    panel = noise(keys[1], (NPTS, SKETCH), 1.0, 6.0, ((0, 32),))
    mixing = noise(keys[2], (SKETCH, RANK), SKETCH ** -0.5, 0.5, (), jnp.float32)
    owners_keys = jax.random.split(jax.random.fold_in(keys[3], 1), NPAIRS // PAIRS_DEV)
    owners_turns = jax.random.permutation(jax.random.fold_in(keys[3], 3), NPAIRS // PAIRS_DEV)
    owners = jax.vmap(lambda own, number: deal_out(jax.random.fold_in(keys[3], 2), own, number, PAIRS_DEV, DEVICES, 1, CAP, 2))(owners_keys, owners_turns).reshape((NPAIRS, 1))
    leaf_picks = plant(jax.random.randint(keys[4], (NPAIRS, 2), 0, PT_DEV // LEAF), jax.random.fold_in(keys[4], 1), 0, (PT_DEV // LEAF) - 1).astype(jnp.int32)
    return {"coords": coords, "panel": panel, "mixing": mixing, "owners": owners, "leaf_picks": leaf_picks}


epsilon = 1e-06

def kernel_tile(left, right):
    highest = lax.Precision.HIGHEST
    left_sq = lax.optimization_barrier(jnp.sum(left * left, axis=0))
    right_sq = lax.optimization_barrier(jnp.sum(right * right, axis=0))
    inner_prod = jnp.einsum('dn,dm->nm', left, right, precision=highest)
    squared = left_sq[:, None] + right_sq[None, :] - 2.0 * inner_prod
    return jnp.exp(squared * (-2.0 / left.shape[0])).astype(jnp.bfloat16)

def make_bases(sketch_rows, mixing):
    highest = lax.Precision.HIGHEST
    narrow = jnp.einsum('lps,sr->lpr', sketch_rows, mixing, precision=highest)
    gram = jnp.einsum('lpr,lpq->lrq', narrow, narrow, precision=highest)
    scale = jnp.sqrt(lax.optimization_barrier(jnp.sum(gram * gram, axis=(1, 2))) + epsilon)
    iterate = gram / scale[:, None, None]
    ident = jnp.broadcast_to(jnp.eye(gram.shape[-1], dtype=gram.dtype), gram.shape)
    root = ident
    for sweep in range(NSWEEPS):
        factor = 1.5 * ident - 0.5 * jnp.einsum('lab,lbc->lac', root, iterate, precision=highest)
        iterate = jnp.einsum('lab,lbc->lac', iterate, factor, precision=highest)
        root = jnp.einsum('lab,lbc->lac', factor, root, precision=highest)
    basis = jnp.einsum('lpr,lrq->lpq', narrow, root, precision=highest) / jnp.sqrt(scale)[:, None, None]
    return basis.astype(jnp.bfloat16)

def reference(coords, panel, mixing, owners, leaf_picks):
    points = coords
    step_rows = math.gcd(NPTS, 512)
    blocks = points.reshape(DIM, NPTS // step_rows, step_rows).transpose(1, 0, 2)

    def one_block(block):
        return jnp.dot(kernel_tile(block, points), panel, preferred_element_type=jnp.float32)
    sketch = lax.map(one_block, blocks).reshape(NPTS, SKETCH)
    bases = make_bases(sketch.reshape(NLEAVES, LEAF, SKETCH), mixing)
    flat_bases = bases.reshape(NLEAVES, LEAF * RANK)
    pair_ids = jnp.arange(NPAIRS, dtype=jnp.int32)
    near = pair_ids // PAIRS_DEV * LEAVES_DEV + leaf_picks[:, 0]
    far = owners[:, 0] * LEAVES_DEV + leaf_picks[:, 1]
    group = math.gcd(NPAIRS, 64)

    def slice_leaf(offset):
        return lax.dynamic_slice_in_dim(points, (offset * LEAF).astype(jnp.int32), LEAF, 1)

    def couple(items):
        near_ids, far_ids = items
        near_pts = jax.vmap(slice_leaf)(near_ids)
        far_pts = jax.vmap(slice_leaf)(far_ids)
        kernels = jax.vmap(kernel_tile)(near_pts, far_pts)
        left = bases[near_ids].astype(jnp.float32)
        right = bases[far_ids].astype(jnp.float32)
        middle = jnp.einsum('gab,gbr->gar', kernels.astype(jnp.float32), right).astype(jnp.bfloat16)
        blocks_out = jnp.einsum('gar,gaq->grq', left, middle.astype(jnp.float32))
        return blocks_out.reshape(group, RANK * RANK)
    couplings = lax.map(couple, (near.reshape(-1, group), far.reshape(-1, group)))
    return (flat_bases, couplings.reshape(NPAIRS, RANK * RANK))
```

```python
import functools
import math

import jax
import jax.numpy as jnp
import numpy as np
from jax import lax
from jax.experimental import pallas as pl
from jax.experimental.pallas import tpu as pltpu
from jax.sharding import PartitionSpec as P

LEAF = 256
RANK = 64
NSWEEPS = 6
EPSILON = 1e-06
DEPTH = 128

F32 = jnp.float32
BF16 = jnp.bfloat16
HIGHEST = lax.Precision.HIGHEST
VMEM = pltpu.VMEM
ANY = pl.ANY


def vmem(count):
    return [pl.BlockSpec(memory_space=VMEM)] * count


def split(value):
    first = value.astype(BF16)
    rest = value - first.astype(F32)
    second = rest.astype(BF16)
    third = (rest - second.astype(F32)).astype(BF16)
    return first.astype(F32), second.astype(F32), third.astype(F32)


def features(points, left):
    dim, count = points.shape
    factor = -2.0 / dim * math.log2(math.e)
    norm = factor * jnp.sum(points * points, axis=0, keepdims=True)
    n1, n2, n3 = (jnp.broadcast_to(part, (dim, count)) for part in split(norm))
    v1, v2, v3 = split(points if left else (-2.0 * factor) * points)
    at = lax.broadcasted_iota(jnp.int32, (dim, count), 0)
    base = 0 if left else 3
    ones = jnp.where((at >= 3 - base) & (at < 6 - base), 1.0, 0.0)
    norms = jnp.where(at == base, n1, jnp.where(at == base + 1, n2, jnp.where(at == base + 2, n3, ones)))
    rows = [v1, v1, v2, v2, v1, v3, norms] if left else [v1, v2, v1, v2, v3, v1, norms]
    pad = jnp.zeros((DEPTH - dim * len(rows), count), F32)
    return jnp.concatenate(rows + [pad], axis=0)


def project_kernel(panel_ref, mixing_ref, out_ref):
    value = jnp.dot(panel_ref[...].astype(F32), mixing_ref[...], precision=HIGHEST, preferred_element_type=F32)
    high = value.astype(BF16)
    low = (value - high.astype(F32)).astype(BF16)
    out_ref[...] = jnp.concatenate([high, low], axis=1)


def project(panel, mixing):
    return pl.pallas_call(
        project_kernel,
        out_shape=jax.ShapeDtypeStruct((panel.shape[0], 2 * mixing.shape[1]), BF16),
        in_specs=vmem(2),
        out_specs=pl.BlockSpec(memory_space=VMEM),
        name="project",
    )(panel, mixing)


def prepare_kernel(row_chunks, own, starts_ref, coords_ref, left_ref, right_ref, points, sems):
    total = points.shape[0]
    copies = []
    for k in range(total):
        start = pl.multiple_of(starts_ref[k], own)
        copies.append(pltpu.make_async_copy(coords_ref.at[:, pl.ds(start, own)], points.at[k], sems.at[k]))
        copies[-1].start()
    for k in range(total):
        copies[k].wait()
        if k < row_chunks:
            left_ref[k * own:(k + 1) * own, :] = features(points[k], True).T.astype(BF16)
        else:
            at = (k - row_chunks) * own
            right_ref[:, at:at + own] = features(points[k], False).astype(BF16)


def prepare(coords, starts, row_chunks, own):
    total = starts.shape[0]
    return pl.pallas_call(
        functools.partial(prepare_kernel, row_chunks, own),
        out_shape=(
            jax.ShapeDtypeStruct((row_chunks * own, DEPTH), BF16),
            jax.ShapeDtypeStruct((DEPTH, (total - row_chunks) * own), BF16),
        ),
        grid_spec=pltpu.PrefetchScalarGridSpec(
            num_scalar_prefetch=1,
            grid=(1,),
            in_specs=[pl.BlockSpec(memory_space=ANY)],
            out_specs=vmem(2),
            scratch_shapes=[VMEM((total, coords.shape[0], own), F32), pltpu.SemaphoreType.DMA((total,))],
        ),
        name="prepare",
    )(starts, coords)


def sketch_kernel(at, first, last, tile, *refs):
    left_ref, right_ref = refs[:2]
    refs = refs[2:]
    total_ref = None
    if not first:
        total_ref, refs = refs[0], refs[1:]
    outs = refs[len(at):]
    panels = refs[:len(at)]
    width = panels[0].shape[1]

    def one(step, out_ref, lead):
        rows = pl.ds(pl.multiple_of(lead + step * tile, tile), tile)
        left = left_ref[rows, :]
        total = jnp.zeros((tile, width), F32) if first else total_ref[rows, :]
        for k, panel_ref in zip(at, panels):
            count = panel_ref.shape[0]
            power = jnp.dot(left, right_ref[:, k * count:(k + 1) * count], preferred_element_type=F32)
            kernel = jnp.exp2(power).astype(BF16)
            total = total + jnp.dot(kernel, panel_ref[...], preferred_element_type=F32)
        if not last:
            out_ref[rows, :] = total
            return 0
        half = width // 2
        total = total + pltpu.roll(total, half, 1)
        lanes = lax.broadcasted_iota(jnp.int32, (LEAF, width), 1)
        out_ref[...] = jnp.where(lanes < half, total[:LEAF], total[LEAF:])
        return 0

    if last:
        for m, out_ref in enumerate(outs):
            one(0, out_ref, m * tile)
    else:
        lax.fori_loop(0, left_ref.shape[0] // tile, lambda step, _: one(step, outs[0], 0), 0)


def sketch(left, right, total, at, panels, last):
    own, width = panels[0].shape
    first = total is None
    if last:
        shapes = [jax.ShapeDtypeStruct((LEAF, width), F32)] * (left.shape[0] // own)
    else:
        shapes = [jax.ShapeDtypeStruct((left.shape[0], width), F32)]
    args = [left, right] + ([] if first else [total]) + list(panels)
    entries = left.shape[0] * own * len(at)
    return pl.pallas_call(
        functools.partial(sketch_kernel, tuple(at), first, last, own),
        out_shape=shapes,
        in_specs=vmem(len(args)),
        out_specs=vmem(len(shapes)),
        cost_estimate=pl.CostEstimate(flops=2 * entries * (DEPTH + width), bytes_accessed=3 << 20, transcendentals=entries),
        name="sketch",
    )(*args)


def bases_kernel(*refs):
    parts, (natural_ref, turned_ref, store) = refs[:-3], refs[-3:]
    narrow = parts[0][...]
    for part in parts[1:]:
        narrow = narrow + part[...]
    width = narrow.shape[1]

    def times(a, b):
        return jnp.dot(a, b, precision=HIGHEST, preferred_element_type=F32)

    gram = lax.dot_general(narrow, narrow, (((0,), (0,)), ((), ())), precision=HIGHEST, preferred_element_type=F32)
    row = lax.broadcasted_iota(jnp.int32, (width, width), 0)
    column = lax.broadcasted_iota(jnp.int32, (width, width), 1)
    gram = jnp.where((row < RANK) == (column < RANK), gram, 0.0)
    sums = jnp.sum(gram * gram, axis=0, keepdims=True)
    lane = lax.broadcasted_iota(jnp.int32, (1, width), 1)
    low = jnp.sum(jnp.where(lane < RANK, sums, 0.0), axis=1, keepdims=True)
    high = jnp.sum(jnp.where(lane < RANK, 0.0, sums), axis=1, keepdims=True)
    scale = jnp.sqrt(jnp.where(lane < RANK, low, high) + EPSILON)
    ident = jnp.where(row == column, 1.0, 0.0)
    iterate = gram / scale
    root = ident
    for sweep in range(NSWEEPS):
        factor = 1.5 * ident - 0.5 * (iterate if sweep == 0 else times(root, iterate))
        if sweep < NSWEEPS - 1:
            iterate = times(iterate, factor)
        root = factor if sweep == 0 else times(factor, root)
    bases = times(narrow, root) / jnp.sqrt(scale)
    turned_ref[...] = bases.T.astype(BF16)
    store[...] = bases
    even = store[pl.ds(0, LEAF // 2, stride=2), :]
    odd = store[pl.ds(1, LEAF // 2, stride=2), :]
    lanes = lax.broadcasted_iota(jnp.int32, even.shape, 1)
    natural_ref[0] = jnp.where(lanes < RANK, even, pltpu.roll(odd, RANK, 1)).astype(BF16)
    natural_ref[1] = jnp.where(lanes < RANK, pltpu.roll(even, RANK, 1), odd).astype(BF16)


def make_bases(parts):
    width = parts[0].shape[1]
    return pl.pallas_call(
        bases_kernel,
        out_shape=(
            jax.ShapeDtypeStruct((width // RANK, LEAF // 2, 2 * RANK), BF16),
            jax.ShapeDtypeStruct((width, LEAF), BF16),
        ),
        in_specs=vmem(len(parts)),
        out_specs=vmem(2),
        scratch_shapes=[VMEM((LEAF, width), F32)],
        name="bases",
    )(*parts)


def tiles_kernel(own, near_ref, far_ref, coords_ref, _, out_ref, near_points, far_points, left_ref, right_ref, sems):
    pairs = out_ref.shape[0]
    near_copy = pltpu.make_async_copy(
        coords_ref.at[:, pl.ds(pl.multiple_of(near_ref[pairs], own), own)], near_points, sems.at[pairs]
    )
    near_copy.start()
    copies = []
    for k in range(pairs):
        start = pl.multiple_of(far_ref[k], LEAF)
        copies.append(pltpu.make_async_copy(coords_ref.at[:, pl.ds(start, LEAF)], far_points.at[k], sems.at[k]))
        copies[-1].start()
    near_copy.wait()
    left_ref[...] = features(near_points[...], True).T.astype(BF16)
    for k in range(pairs):
        copies[k].wait()

    def one(k, _):
        left = left_ref[pl.ds(pl.multiple_of(near_ref[k] * LEAF, LEAF), LEAF), :]
        right = features(far_points[k], False).astype(BF16)
        out_ref[k] = jnp.exp2(jnp.dot(left, right, preferred_element_type=F32)).astype(BF16)
        return 0

    lax.fori_loop(0, pairs, one, 0)


def make_tiles(coords, near, far, own, after):
    pairs = far.shape[0]
    return pl.pallas_call(
        functools.partial(tiles_kernel, own),
        out_shape=jax.ShapeDtypeStruct((pairs, LEAF, LEAF), BF16),
        grid_spec=pltpu.PrefetchScalarGridSpec(
            num_scalar_prefetch=2,
            grid=(1,),
            in_specs=[pl.BlockSpec(memory_space=ANY), pl.BlockSpec(memory_space=ANY)],
            out_specs=pl.BlockSpec(memory_space=VMEM),
            scratch_shapes=[
                VMEM((coords.shape[0], own), F32),
                VMEM((pairs, coords.shape[0], LEAF), F32),
                VMEM((own, DEPTH), BF16),
                VMEM((DEPTH, LEAF), BF16),
                pltpu.SemaphoreType.DMA((pairs + 1,)),
            ],
        ),
        name="tiles",
    )(near, far, coords, after)


def couple_kernel(count, near_ref, source_ref, offset_ref, tiles_ref, own_ref, *refs):
    sources, (out_ref, far, sems) = refs[:count], refs[count:]
    pairs = out_ref.shape[0]

    def copy(k, index):
        rows = pl.ds(pl.multiple_of(offset_ref[k], RANK), RANK)
        return pltpu.make_async_copy(sources[index].at[rows, :], far.at[k], sems.at[k])

    def begin(k, _):
        for index in range(count):
            @pl.when(source_ref[k] == index)
            def _():
                copy(k, index).start()
        return 0

    lax.fori_loop(0, pairs, begin, 0)

    def one(k, _):
        copy(k, 0).wait()
        middle = lax.dot_general(tiles_ref[k], far[k], (((1,), (1,)), ((), ())), preferred_element_type=F32)
        left = own_ref[pl.ds(pl.multiple_of(near_ref[k] * RANK, RANK), RANK), :]
        out_ref[k] = jnp.dot(left, middle.astype(BF16), preferred_element_type=F32)
        return 0

    lax.fori_loop(0, pairs, one, 0)


def couple(near, source, offset, tiles, own, sources):
    pairs = offset.shape[0]
    return pl.pallas_call(
        functools.partial(couple_kernel, len(sources)),
        out_shape=jax.ShapeDtypeStruct((pairs, RANK, RANK), F32),
        grid_spec=pltpu.PrefetchScalarGridSpec(
            num_scalar_prefetch=3,
            grid=(1,),
            in_specs=vmem(2) + [pl.BlockSpec(memory_space=ANY)] * len(sources),
            out_specs=pl.BlockSpec(memory_space=VMEM),
            scratch_shapes=[VMEM((pairs, RANK, LEAF), BF16), pltpu.SemaphoreType.DMA((pairs,))],
        ),
        name="couple",
    )(near, source, offset, tiles, own, *sources)


def per_device(coords, panel, mixing, owners, leaf_picks):
    row_count = lax.axis_size("row")
    col_count = lax.axis_size("col")
    planes = col_count // 2
    row = lax.axis_index("row")
    col = lax.axis_index("col")
    own = panel.shape[0]
    leaves = own // LEAF

    def swap(value, axis, mask):
        return lax.ppermute(value, axis, [(i, i ^ mask) for i in range(lax.axis_size(axis))])

    columns = [(0, 0), (0, 1)] + [(m, 0) for m in range(1, row_count)] + [(m, 1) for m in range(1, row_count)]
    masks = np.array([(0, 2 * m) for m in range(planes)] + columns, np.int32)
    starts = ((row ^ masks[:, 0]) * col_count + (col ^ masks[:, 1])) * own

    mixed = project(panel, mixing)
    partner = swap(mixed, "col", 1)
    along = [swap(mixed, "row", m) for m in range(1, row_count)]
    left, right = prepare(coords, starts, planes, own)
    (total,) = sketch(left, right, None, [0, 1], [mixed, partner], False)
    stacked = jnp.concatenate(along, axis=0)
    crossed = swap(stacked, "col", 1).reshape((row_count - 1, own, mixed.shape[1]))
    (total,) = sketch(left, right, total, range(2, 1 + row_count), along, False)
    parts = sketch(
        left, right, total, range(1 + row_count, 2 * row_count), [crossed[m] for m in range(row_count - 1)], True
    )
    narrow = [parts[0]] + [swap(parts[m], "col", 2 * m) for m in range(1, planes)]
    natural, turned = make_bases(narrow)

    owner = owners[:, 0]
    owner_row, owner_col = owner // col_count, owner % col_count
    near_start = ((row * col_count + col) * own)[None]
    near = jnp.concatenate([leaf_picks[:, 0], near_start.astype(jnp.int32)])
    far_start = (owner * leaves + leaf_picks[:, 1]) * LEAF
    away = owner_col ^ col
    source = (away % 2) * planes + away // 2
    offset = ((owner_row ^ row) * leaves + leaf_picks[:, 1]) * RANK

    line = jnp.concatenate([turned] + [swap(turned, "row", m) for m in range(1, row_count)], axis=0)
    near_side = [line] + [swap(line, "col", 2 * m) for m in range(1, planes)]
    far_side = [swap(value, "col", 1) for value in near_side]
    tiles = make_tiles(coords, near, far_start, own, turned)
    blocks = couple(near, source, offset, tiles, turned, near_side + far_side)
    return natural.reshape(leaves, LEAF * RANK), blocks.reshape(owner.shape[0], RANK * RANK)


def solution(mesh):
    spread = P(("row", "col"), None)
    return jax.shard_map(
        per_device,
        mesh=mesh,
        in_specs=(P(), spread, P(), spread, spread),
        out_specs=(spread, spread),
        check_vma=False,
    )
```
